512 devices in a mesh: grp: 4 (over z_lo, core), blk: 128 (over y, z_hi, x).
Axes of the slice: x: 4, y: 8, z: 8 (z_hi: 4, z_lo: 2; z = z_hi * 2 + z_lo), core: 2. Of those that a mesh axis runs over, the one named last changes fastest.
Arguments:
- vertices: float32 [3, 131072], P(None, ('grp', 'blk')), may hold values from -6 to 6
- faces: int32 [3, 262144], P(None, ('grp', 'blk')), may hold values from 0 to 255
- trial_step: float32 [3, 131072], P(None, ('grp', 'blk')), may hold values from -2 to 2
- accepted: int32 [4], P('grp'), may hold values from 0 to 1
- face_weight: float32 [262144], P(('grp', 'blk')), may hold values from 0.5 to 6
- partner_shift: int32 [2, 4], replicated, may hold values from 1 to 3, as said below
Outputs:
- vertex_grad: float32 [3, 131072], P(None, ('grp', 'blk'))
- energy: float32 [1], replicated
The draws below stay inside these ranges and needn't reach their ends.
Inputs may be any that keep to these rules, and one draw needn't show every extreme that they name: `partner_shift`: for each group the 2 offsets are all different, and the first round's offset is 4 // 2 for every group.
All inputs are finite; a program needn't handle non-finite values.
Results may differ from the reference program's by a relative error of at most 0.0001.
Values sent between devices are 32-bit elements; how exact they have to be, the bound alone decides.
A program may use at most 64 MiB of HBM per device.

```python
import jax
import jax.numpy as jnp
from jax import lax

FACES_DEV = 512
VERT_DEV = 256
HOPS = 4
ROUNDS = 2
FACES = 262144
VERTS = 131072
N_GRP = 4
N_BLK = 128


def draw_face_weight(key, part):
    total = FACES_DEV * N_GRP * N_BLK
    base = jnp.exp(jax.random.uniform(key, (total,), jnp.float32, jnp.log(0.5), jnp.log(2.0)))
    owner = (jnp.arange(total) // FACES_DEV).astype(jnp.float32)
    rise = 1.0 + 2.0 * owner / max(N_GRP * N_BLK - 1, 1)
    return base * rise


def draw_partner_shift(key, part):
    half = N_GRP // 2
    others = jnp.array([s for s in range(1, N_GRP) if s != half], jnp.int32)
    keys = jax.random.split(jax.random.fold_in(key, 41), N_GRP)

    def pick(one_key):
        return jax.random.permutation(one_key, others)[:ROUNDS - 1]
    rest = jax.vmap(pick)(keys).astype(jnp.int32)
    first = jnp.full((1, N_GRP), half, jnp.int32)
    return jnp.concatenate([first, rest.T], 0).astype(jnp.int32)


def touch_ends(result, stream_key, least, high):
    index_at = [jax.random.randint(jax.random.fold_in(stream_key, axis), (), 0, length) for axis, length in enumerate(result.shape)]
    longest = result.shape.index(max(result.shape))
    neighbour = index_at[:longest] + [(index_at[longest] + 1) % result.shape[longest]] + index_at[longest + 1:]
    return result.at[tuple(index_at)].set(least).at[tuple(neighbour)].set(high)


def block_levels(stream_key, extent, shards, least, largest):
    def one(axis_at, shards_of):
        steps = jax.random.uniform(jax.random.fold_in(jax.random.fold_in(stream_key, 6), axis_at), (shards_of,), jnp.float32, least / len(shards), largest / len(shards))
        return jnp.repeat(jnp.exp(steps), extent[axis_at] // shards_of).reshape((-1,) + (1,) * (len(extent) - axis_at - 1))

    gain = one(*shards[0])
    for cut in shards[1:]:
        gain = gain * one(*cut)
    return gain


def scatter_about(key, shape, width, reach, shards=(), kind=jnp.bfloat16):
    values = jax.random.normal(key, shape, jnp.float32) * width
    if len(shards) > 0:
        values = block_levels(key, shape, shards, -0.22, 0.18) * values
    return jnp.clip(values, min=-reach, max=reach).astype(kind)


def setup_inputs(seed: int = 0) -> dict:
    key_of = jax.random.split(jax.random.key(seed), 7)
    vertices = scatter_about(key_of[0], (3, VERTS), 1.0, 6.0, ((1, 512),), jnp.float32)
    faces = touch_ends(jax.random.randint(key_of[1], (3, FACES), 0, VERT_DEV), jax.random.fold_in(key_of[1], 1), 0, VERT_DEV - 1).astype(jnp.int32)
    trial_step = scatter_about(key_of[2], (3, VERTS), 0.3, 2.0, ((1, 512),), jnp.float32)
    accepted = touch_ends(jax.random.randint(key_of[3], (N_GRP,), 0, 2), jax.random.fold_in(key_of[3], 1), 0, 1).astype(jnp.int32)
    face_weight = draw_face_weight(jax.random.fold_in(key_of[6], 71), 0)
    partner_shift = draw_partner_shift(jax.random.fold_in(key_of[6], 71), 0)
    return {"vertices": vertices, "faces": faces, "trial_step": trial_step, "accepted": accepted, "face_weight": face_weight, "partner_shift": partner_shift}


EPS2 = 0.05

def pair_energy(own_geo, own_weight, other_geo, other_weight):
    d0 = own_geo[0][:, None] - other_geo[0][None, :]
    d1 = own_geo[1][:, None] - other_geo[1][None, :]
    d2 = own_geo[2][:, None] - other_geo[2][None, :]
    dist = d0 * d0 + d1 * d1 + d2 * d2 + EPS2
    proj_own = own_geo[3][:, None] * d0 + own_geo[4][:, None] * d1 + own_geo[5][:, None] * d2
    proj_other = other_geo[3][None, :] * d0 + other_geo[4][None, :] * d1 + other_geo[5][None, :] * d2
    kernel = own_weight[:, None] * other_weight[None, :] * (proj_own * proj_own + proj_other * proj_other) / (dist * dist)
    return jnp.sum(kernel)

def tile_grads(own, other):

    def energy_of(first, second):
        return pair_energy(first, own[6], second, other[6])
    value, pullback = jax.vjp(energy_of, own[:6], other[:6])
    grad_own, grad_other = pullback(jnp.ones_like(value))
    return (value, grad_own, grad_other)

def geometry(pos, tri):
    first = pos[:, tri[0]]
    second = pos[:, tri[1]]
    third = pos[:, tri[2]]
    center = (first + second + third) / 3.0
    normal = 0.5 * jnp.cross(second - first, third - first, axis=0)
    return jnp.concatenate([center, normal], 0)

def reference(vertices, faces, trial_step, accepted, face_weight, partner_shift):
    devices = N_GRP * N_BLK
    step_on = jnp.repeat(accepted.astype(vertices.dtype), N_BLK * VERT_DEV)
    pos = vertices + step_on[None, :] * trial_step
    owner = jnp.arange(FACES, dtype=jnp.int32) // FACES_DEV * VERT_DEV
    tri = faces + owner[None, :]

    def geo_of(p):
        return geometry(p, tri)
    geo, pull = jax.vjp(geo_of, pos)
    data = jnp.concatenate([geo, face_weight[None, :].astype(geo.dtype)], 0)
    blocks = data.reshape(7, N_GRP, N_BLK, FACES_DEV).transpose(1, 2, 0, 3)

    def visit(index, carry):
        energy, grads = carry
        g = index // N_BLK
        b = index % N_BLK
        own = blocks[g, b]
        value, grad_a, grad_b = tile_grads(own, own)
        energy = energy + 0.5 * value
        grads = grads.at[g, b].add(0.5 * (grad_a + grad_b))
        for k in range(1, HOPS + 1):
            later = (b + k) % N_BLK
            value, grad_a, grad_b = tile_grads(own, blocks[g, later])
            energy = energy + value
            grads = grads.at[g, b].add(grad_a).at[g, later].add(grad_b)
        for r in range(ROUNDS):
            other_group = (g + partner_shift[r, g]) % N_GRP
            value, grad_a, grad_b = tile_grads(own, blocks[other_group, b])
            energy = energy + value
            grads = grads.at[g, b].add(grad_a).at[other_group, b].add(grad_b)
        return (energy, grads)
    init = (jnp.zeros((), geo.dtype), jnp.zeros((N_GRP, N_BLK, 6, FACES_DEV), geo.dtype))
    energy, grads = lax.fori_loop(0, N_GRP * N_BLK, visit, init)
    face_grad = grads.transpose(2, 0, 1, 3).reshape(6, FACES)
    vertex_grad = pull(face_grad)[0] / FACES_DEV
    total = energy / (FACES_DEV * FACES_DEV * devices)
    return (vertex_grad, total.reshape(1))
```

```python
import functools

import jax
import jax.numpy as jnp
from jax import lax
from jax.experimental import pallas as pl
from jax.experimental.pallas import tpu as pltpu
from jax.sharding import PartitionSpec as P

F = jnp.float32
B = jnp.bfloat16
EPS2 = 0.05
HOPS = 4
CHUNK = 128
LANES = 256
ROWS = 16
MESH = pl.DeviceIdType.MESH

TILES = (
    [("grp", 2), ("grp", 1)]
    + [("blk", k) for k in range(1, HOPS + 1)]
    + [("grp", 3)]
    + [("blk", -k) for k in range(1, HOPS + 1)]
)
HALF_AT = 2
FULL_AT = 7
Y, ZH, X, G = 8, 4, 4, 4


def split3(x):
    h = x.astype(B).astype(F)
    r = x - h
    m = r.astype(B).astype(F)
    return h, m, r - m


def dot(a, b):
    return jnp.dot(a, b, preferred_element_type=F)


def cross(a, b):
    return [
        a[1] * b[2] - a[2] * b[1],
        a[2] * b[0] - a[0] * b[2],
        a[0] * b[1] - a[1] * b[0],
    ]


def rows_of(x, n=3):
    return [x[k : k + 1] for k in range(n)]


def own_prep(own, ra, rb, cj):
    n = own.shape[1]
    z = jnp.zeros((1, n), F)
    ya = jnp.concatenate([-own[3:6], z, z, z, own[7:8], z], 0)
    yb = jnp.concatenate([z, z, z, own[0:3], z, z - 1.0], 0)
    for y, r in ((ya, ra), (yb, rb)):
        h, m, low = split3(y)
        r[...] = jnp.concatenate([h, m, low, h, m, h], 0).astype(B)
    for k in range(3):
        cj[k] = jnp.broadcast_to(own[k : k + 1], (8, n))


def other_prep(blk, wrow, xt, ct, fs):
    row = lax.broadcasted_iota(jnp.int32, blk.shape, 0)
    x = jnp.where(row == 6, 1.0, blk)
    h, m, low = split3(x)
    tr = jnp.concatenate([h, h, h, m, m, low, blk, blk], 0).T
    xt[...] = tr[:, :48].astype(B)
    ct[...] = tr[:, 48:56]
    h, m, low = split3(x * wrow)
    fs[...] = jnp.concatenate([h, m, low, jnp.zeros_like(low)], 0).astype(B)


def pairs(ct, cj, ab, co, slot, base, r0):
    n = cj.shape[2]
    rows = slice(base + r0, base + r0 + ROWS)
    cr = slice(r0, r0 + ROWS)
    for l0 in range(0, n, LANES):
        ls = slice(l0, l0 + LANES)
        d = []
        for k in range(3):
            other = jnp.broadcast_to(ct[rows, k : k + 1], (ROWS, LANES))
            own = cj[k, :, ls]
            d.append(jnp.concatenate([own] * (ROWS // 8), 0) - other)
        q = 1.0 / ((d[0] * d[0] + EPS2) + (d[1] * d[1] + d[2] * d[2]))
        q2 = q * q
        a = ab[slot, 0, cr, ls]
        b = ab[slot, 1, cr, ls]
        al = a * q2
        be = b * q2
        ga = (a * al + b * be) * q
        for m, v in enumerate((al, be, ga)):
            h = v.astype(B)
            co[slot, 2 * m, cr, ls] = h
            co[slot, 2 * m + 1, cr, ls] = (v - h.astype(F)).astype(B)


def tile(xt, ct, fs, ra, rb, cj, ab, co, acc):
    chunks = cj.shape[2] // CHUNK

    def project(c):
        x = xt[c * CHUNK : (c + 1) * CHUNK, :]
        ab[c % 2, 0] = dot(x, ra[...])
        ab[c % 2, 1] = dot(x, rb[...])

    project(0)
    for c in range(chunks):
        if c + 1 < chunks:
            project(c + 1)
        for r0 in range(0, CHUNK, ROWS):
            pairs(ct, cj, ab, co, c % 2, c * CHUNK, r0)
        f = fs[:, c * CHUNK : (c + 1) * CHUNK]
        for m in range(3):
            acc[m] += dot(f, co[c % 2, 2 * m]) + dot(f, co[c % 2, 2 * m + 1])


def sums_of(acc):
    return [acc[m, 0:8, :] + acc[m, 8:16, :] + acc[m, 16:24, :] for m in range(3)]


def grad_normal(own, s):
    return own[0:3] * s[0][6:7] - s[0][0:3]


def energy_of(own, acc):
    s = sums_of(acc)
    e = jnp.sum(own[3:6] * grad_normal(own, s) + own[0:3] * s[1][3:6], 0, keepdims=True)
    e = (e - s[1][7:8]) * own[6:7]
    n = e.shape[1]
    return functools.reduce(jnp.add, [e[:, k : k + 128] for k in range(0, n, 128)])


def kernel(
    ver_ref, faces_ref, step_ref, weight_ref, acc_ref, shift_ref, grad_ref, energy_ref,
    blocks, hot, xt, ct, fs, ra, rb, cj, ab, co, acc, part,
    box_a, box_b, box_c, send, recv, send_a, recv_a, send_b, recv_b, send_c, recv_c,
):
    g = lax.axis_index("grp")
    b = lax.axis_index("blk")
    blk_n = Y * ZH * X
    y, zh, x = b // (ZH * X), (b // X) % ZH, b % X

    def peer_a(i):
        j = (g * ZH + zh + i) % (G * ZH)
        return (j // ZH, (y * ZH + j % ZH) * X + x)

    def peer_b(i):
        return (g, (((y + i) % Y) * ZH + zh) * X + x)

    def peer_c(i):
        return (g, (y * ZH + zh) * X + (x + i) % X)

    def visitor(axis, k):
        if axis == "grp":
            return ((g + G - k) % G, b)
        return (g, (b + blk_n - k) % blk_n)

    peers = [visitor(*t) for t in TILES if t[0] == "blk"]
    peers += [peer_a(i) for i in range(1, G * ZH)]
    peers += [peer_b(i) for i in range(1, Y)] + [peer_c(i) for i in range(1, X)]
    barrier = pltpu.get_barrier_semaphore()
    for p in peers:
        pl.semaphore_signal(barrier, inc=1, device_id=p, device_id_type=MESH)

    verts, count = ver_ref.shape[1], faces_ref.shape[1]
    pos = ver_ref[...] + acc_ref[0].astype(F) * step_ref[...]
    table = jnp.concatenate([*split3(pos), jnp.zeros((7, verts), F)], 0).astype(B)
    vert = lax.broadcasted_iota(jnp.int32, (verts, count), 0)
    corners = []
    for k in range(3):
        hot[k] = jnp.where(vert == faces_ref[k : k + 1, :], 1.0, 0.0).astype(B)
        u = dot(table, hot[k])
        corners.append(u[0:3] + u[3:6] + u[6:9])
    center = (corners[0] + corners[1] + corners[2]) / 3.0
    e1 = rows_of(corners[1] - corners[0])
    e2 = rows_of(corners[2] - corners[0])
    normal = 0.5 * jnp.concatenate(cross(e1, e2), 0)
    offset = jnp.sum(center * normal, 0, keepdims=True)
    own = jnp.concatenate([center, normal, weight_ref[...], offset], 0)
    blocks[0] = own

    pl.semaphore_wait(barrier, len(peers))

    def block_copy(t, to):
        return pltpu.make_async_remote_copy(
            src_ref=blocks.at[0], dst_ref=blocks.at[t], send_sem=send.at[t - 1],
            recv_sem=recv.at[t - 1], device_id=to, device_id_type=MESH,
        )

    for t, where in enumerate(TILES):
        block_copy(t + 1, visitor(*where)).start()

    own_prep(own, ra, rb, cj)
    acc[...] = jnp.zeros_like(acc)

    def times(k):
        total = jnp.float32(0.0)
        for r in range(shift_ref.shape[0]):
            total += jnp.where(shift_ref[r, g] == k, 1.0, 0.0)
            total += jnp.where(shift_ref[r, (g + k) % G] == G - k, 1.0, 0.0)
        return total

    times_of = {k: times(k) for k in range(1, G)}

    def spread(value, box, send_sem, recv_sem, peer, n):
        box[0] = value
        for i in range(1, n):
            pltpu.make_async_remote_copy(
                src_ref=box.at[0], dst_ref=box.at[i], send_sem=send_sem.at[i - 1],
                recv_sem=recv_sem.at[i - 1], device_id=peer(i), device_id_type=MESH,
            ).start()

    def gathered(box, send_sem, recv_sem, peer, n):
        for i in range(1, n):
            pltpu.make_async_remote_copy(
                src_ref=box.at[0], dst_ref=box.at[i], send_sem=send_sem.at[i - 1],
                recv_sem=recv_sem.at[i - 1], device_id=peer(i), device_id_type=MESH,
            ).wait()
        return functools.reduce(jnp.add, [box[i] for i in range(n)])

    boxes = (
        (box_a, send_a, recv_a, peer_a, G * ZH),
        (box_b, send_b, recv_b, peer_b, Y),
        (box_c, send_c, recv_c, peer_c, X),
    )

    def visit(t, carry):
        @pl.when(t > 0)
        def _():
            block_copy(t, visitor("blk", 1)).wait_recv()

        @pl.when(t == HALF_AT)
        def _():
            part[...] = energy_of(own, acc)

        @pl.when(t == FULL_AT)
        def _():
            spread(energy_of(own, acc) - 0.5 * part[...], *boxes[0])

        @pl.when(t == FULL_AT + 2)
        def _():
            spread(gathered(*boxes[0]), *boxes[1])

        @pl.when(t == FULL_AT + 4)
        def _():
            spread(gathered(*boxes[1]), *boxes[2])

        blk = blocks[t]
        scale = jnp.float32(1.0)
        for i, (axis, k) in enumerate(TILES):
            if axis == "grp":
                scale = jnp.where(t == i + 1, times_of[k], scale)
        other_prep(blk, blk[6:7] * scale, xt, ct, fs)
        tile(xt, ct, fs, ra, rb, cj, ab, co, acc)
        return carry

    lax.fori_loop(0, len(TILES) + 1, visit, 0)

    s = sums_of(acc)
    twice = 2.0 * own[6:7]
    gn = rows_of(grad_normal(own, s) * twice)
    gc = own[3:6] * s[0][6:7] + s[1][3:6] - 2.0 * (own[0:3] * s[2][6:7] - s[2][0:3])
    gc = gc * (twice / 3.0)
    g1 = 0.5 * jnp.concatenate(cross(e2, gn), 0)
    g2 = 0.5 * jnp.concatenate(cross(gn, e1), 0)
    total = jnp.zeros((16, verts), F)
    for k, gu in enumerate((gc - g1 - g2, gc + g1, gc + g2)):
        parts = jnp.concatenate([*split3(gu), jnp.zeros((7, count), F)], 0).astype(B)
        total += lax.dot_general(parts, hot[k], (((1,), (1,)), ((), ())), preferred_element_type=F)
    grad_ref[...] = (total[0:3] + total[3:6] + total[6:9]) * (1.0 / count)

    for t, where in enumerate(TILES):
        block_copy(t + 1, visitor(*where)).wait_send()
    energy_ref[0] = jnp.sum(gathered(*boxes[2])) * (1.0 / (count * count * G * blk_n))


def shards(vertices, faces, trial_step, accepted, face_weight, partner_shift):
    verts, count = vertices.shape[1], faces.shape[1]
    vmem = pl.BlockSpec(memory_space=pltpu.VMEM)
    smem = pl.BlockSpec(memory_space=pltpu.SMEM)
    dma = pltpu.SemaphoreType.DMA
    n = len(TILES)
    return tuple(pl.pallas_call(
        kernel,
        out_shape=(jax.ShapeDtypeStruct((3, verts), F), jax.ShapeDtypeStruct((1,), F)),
        in_specs=[vmem] * 4 + [smem] * 2,
        out_specs=(vmem, smem),
        scratch_shapes=[
            pltpu.VMEM((n + 1, 8, count), F),
            pltpu.VMEM((3, verts, count), B),
            pltpu.VMEM((count, 48), B),
            pltpu.VMEM((count, 8), F),
            pltpu.VMEM((32, count), B),
            pltpu.VMEM((48, count), B),
            pltpu.VMEM((48, count), B),
            pltpu.VMEM((3, 8, count), F),
            pltpu.VMEM((2, 2, CHUNK, count), F),
            pltpu.VMEM((2, 6, CHUNK, count), B),
            pltpu.VMEM((3, 32, count), F),
            pltpu.VMEM((1, 128), F),
            pltpu.VMEM((G * ZH, 1, 128), F),
            pltpu.VMEM((Y, 1, 128), F),
            pltpu.VMEM((X, 1, 128), F),
            dma((n,)), dma((n,)),
            dma((G * ZH - 1,)), dma((G * ZH - 1,)),
            dma((Y - 1,)), dma((Y - 1,)),
            dma((X - 1,)), dma((X - 1,)),
        ],
        compiler_params=pltpu.CompilerParams(collective_id=0, has_side_effects=True),
    )(vertices, faces, trial_step, face_weight.reshape(1, count), accepted, partner_shift))


def solution(mesh):
    both = ("grp", "blk")
    placed = (P(None, both), P(None, both), P(None, both), P("grp"), P(both), P())
    return jax.shard_map(
        shards, mesh=mesh, in_specs=placed, out_specs=(P(None, both), P()), check_vma=False
    )
```

```python
import functools

import jax
import jax.numpy as jnp
from jax import lax
from jax.experimental import pallas as pl
from jax.experimental.pallas import tpu as pltpu
from jax.sharding import PartitionSpec as P

F = jnp.float32
B = jnp.bfloat16
EPS2 = 0.05
HOPS = 4
CHUNK = 256
LANES = 256
ROWS = 16
MESH = pl.DeviceIdType.MESH
Y, ZH, X, G = 8, 4, 4, 4

TILES = (
    [("grp", 2), ("grp", 3)]
    + [("blk", -k) for k in range(1, HOPS + 1)]
    + [("grp", 1)]
    + [("blk", k) for k in range(1, HOPS + 1)]
)
SAVED = 7
COUNT = len(TILES) + 1


def split3(x):
    h = x.astype(B).astype(F)
    r = x - h
    m = r.astype(B).astype(F)
    return h, m, r - m


def dot(a, b):
    return jnp.dot(a, b, preferred_element_type=F)


def cross(a, b):
    return [
        a[1] * b[2] - a[2] * b[1],
        a[2] * b[0] - a[0] * b[2],
        a[0] * b[1] - a[1] * b[0],
    ]


def rows_of(x, n=3):
    return [x[k : k + 1] for k in range(n)]


def own_prep(own, root, ra, rb, cj):
    n = own.shape[1]
    z = jnp.zeros((1, n), F)
    ya = jnp.concatenate([-own[3:6], z, z, z, own[7:8], z], 0)
    yb = jnp.concatenate([z, z, z, own[0:3], z, z - 1.0], 0)
    for y, r in ((ya, ra), (yb, rb)):
        h, m, low = split3(y * root)
        r[...] = jnp.concatenate([h, m, low, h, m, h], 0).astype(B)
    for k in range(3):
        cj[k] = jnp.broadcast_to(own[k : k + 1], (8, n))


def prepare(blk, scale, xt, ct, fs, t):
    row = lax.broadcasted_iota(jnp.int32, blk.shape, 0)
    x = jnp.where(row == 6, 1.0, blk)
    h, m, low = split3(x * jnp.sqrt(blk[6:7] * scale))
    tr = jnp.concatenate([h, h, h, m, m, low, blk, blk], 0).T
    xt[...] = tr[:, :48].astype(B)
    ct[...] = tr[:, 48:56]
    z = jnp.zeros_like(x)
    fs[t] = jnp.concatenate([h, m, low, z, *split3(x), z], 0).astype(B)


def inverse(ct, cj, rows, ls):
    d = []
    for k in range(3):
        other = jnp.broadcast_to(ct[rows, k : k + 1], (ROWS, LANES))
        own = cj[k, :, ls]
        d.append(jnp.concatenate([own] * (ROWS // 8), 0) - other)
    return 1.0 / ((d[0] * d[0] + EPS2) + (d[1] * d[1] + d[2] * d[2]))


def slabs(first, rows, lanes):
    for r0 in range(first, first + rows, ROWS):
        for l0 in range(0, lanes, LANES):
            yield slice(r0, r0 + ROWS), slice(l0, l0 + LANES)


def energy_pass(ct, cj, ab, i, qk, t, eacc):
    n = cj.shape[2]
    e = [eacc[:, k : k + 128] for k in range(0, n, 128)]
    for rows, ls in slabs(0, n, n):
        q = inverse(ct, cj, rows, ls)
        a = ab[i, 0, rows, ls]
        b = ab[i, 1, rows, ls]
        kern = (a * a + b * b) * (q * q)
        qk[t, 0, rows, ls] = q
        qk[t, 1, rows, ls] = kern
        for k in range(0, LANES, 128):
            for r in range(0, ROWS, 8):
                e[(ls.start + k) // 128] += kern[r : r + 8, k : k + 128]
    for k, v in enumerate(e):
        eacc[:, k * 128 : (k + 1) * 128] = v


def store_parts(co, c, cr, ls, values):
    for m, v in enumerate(values):
        h = v.astype(B)
        co[c, 2 * m, cr, ls] = h
        co[c, 2 * m + 1, cr, ls] = (v - h.astype(F)).astype(B)


def reduce_chunk(co, c, fs, t, acc):
    ks = slice(c * CHUNK, (c + 1) * CHUNK)
    for m in range(3):
        first = 32 if m == 2 else 0
        f = fs[t, first : first + 32, ks]
        acc[m] += dot(f, co[c, 2 * m]) + dot(f, co[c, 2 * m + 1])


def grad_pass(values, co, fs, t, before, acc, n):
    chunks = n // CHUNK
    for c in range(chunks):
        for rows, ls in slabs(c * CHUNK, CHUNK, n):
            cr = slice(rows.start - c * CHUNK, rows.stop - c * CHUNK)
            store_parts(co, c, cr, ls, values(rows, ls))
        if c == 0:
            reduce_chunk(co, chunks - 1, fs, before, acc)
        else:
            reduce_chunk(co, c - 1, fs, t, acc)


def saved_values(ab, i, qk, t):
    def values(rows, ls):
        q = qk[t, 0, rows, ls]
        q2 = q * q
        return ab[i, 0, rows, ls] * q2, ab[i, 1, rows, ls] * q2, qk[t, 1, rows, ls] * q

    return values


def full_values(ct, cj, ab, i):
    def values(rows, ls):
        q = inverse(ct, cj, rows, ls)
        q2 = q * q
        a = ab[i, 0, rows, ls]
        b = ab[i, 1, rows, ls]
        al = a * q2
        be = b * q2
        return al, be, (a * al + b * be) * q

    return values


def kernel(
    ver_hbm, faces_hbm, step_hbm, weight_hbm, acc_hbm, shift_hbm, grad_ref, energy_ref,
    ver_ref, faces_ref, step_ref, weight_ref, acc_ref, shift_ref, in_sem,
    blocks, hot, xt0, xt1, ct0, ct1, fs, ra, rb, cj, ab0, ab1, qk, co, acc, eacc,
    box_a, box_b, box_c, send, recv, send_a, recv_a, send_b, recv_b, send_c, recv_c,
):
    g = lax.axis_index("grp")
    b = lax.axis_index("blk")
    blk_n = Y * ZH * X
    y, zh, x = b // (ZH * X), (b // X) % ZH, b % X

    def peer_a(i):
        j = (g * ZH + zh + i) % (G * ZH)
        return (j // ZH, (y * ZH + j % ZH) * X + x)

    def peer_b(i):
        return (g, (((y + i) % Y) * ZH + zh) * X + x)

    def peer_c(i):
        return (g, (y * ZH + zh) * X + (x + i) % X)

    def visitor(axis, k):
        if axis == "grp":
            return ((g + G - k) % G, b)
        return (g, (b + blk_n - k) % blk_n)

    peers = [visitor(*t) for t in TILES if t[0] == "blk"]
    peers += [peer_a(i) for i in range(1, G * ZH)]
    peers += [peer_b(i) for i in range(1, Y)] + [peer_c(i) for i in range(1, X)]
    barrier = pltpu.get_barrier_semaphore()
    for p in peers:
        pl.semaphore_signal(barrier, inc=1, device_id=p, device_id_type=MESH)

    loads = [
        pltpu.make_async_copy(src, dst, in_sem.at[i])
        for i, (src, dst) in enumerate((
            (ver_hbm, ver_ref), (step_hbm, step_ref), (faces_hbm, faces_ref),
            (weight_hbm, weight_ref), (acc_hbm, acc_ref), (shift_hbm, shift_ref),
        ))
    ]
    for c in loads:
        c.start()
    acc[...] = jnp.zeros_like(acc)
    eacc[...] = jnp.zeros_like(eacc)
    co[co.shape[0] - 1] = jnp.zeros(co.shape[1:], B)
    for c in loads:
        c.wait()

    verts, count = ver_ref.shape[1], faces_ref.shape[1]
    pos = ver_ref[...] + acc_ref[0].astype(F) * step_ref[...]
    table = jnp.concatenate([*split3(pos), jnp.zeros((7, verts), F)], 0).astype(B)
    vert = lax.broadcasted_iota(jnp.int32, (verts, count), 0)
    corners = []
    for k in range(3):
        hot[k] = jnp.where(vert == faces_ref[k : k + 1, :], 1.0, 0.0).astype(B)
        u = dot(table, hot[k])
        corners.append(u[0:3] + u[3:6] + u[6:9])
    center = (corners[0] + corners[1] + corners[2]) / 3.0
    e1 = rows_of(corners[1] - corners[0])
    e2 = rows_of(corners[2] - corners[0])
    normal = 0.5 * jnp.concatenate(cross(e1, e2), 0)
    offset = jnp.sum(center * normal, 0, keepdims=True)
    own = jnp.concatenate([center, normal, weight_ref[...], offset], 0)
    blocks[0] = own

    pl.semaphore_wait(barrier, len(peers))

    def block_copy(t, to):
        return pltpu.make_async_remote_copy(
            src_ref=blocks.at[0], dst_ref=blocks.at[t], send_sem=send.at[t - 1],
            recv_sem=recv.at[t - 1], device_id=to, device_id_type=MESH,
        )

    for t in reversed(range(1, SAVED)):
        block_copy(t, visitor(*TILES[t - 1])).start()
    for t in range(SAVED, COUNT):
        block_copy(t, visitor(*TILES[t - 1])).start()

    root = jnp.sqrt(own[6:7])
    own_prep(own, root, ra, rb, cj)

    def times(k):
        total = jnp.float32(0.0)
        for r in range(shift_ref.shape[0]):
            total += jnp.where(shift_ref[r, g] == k, 1.0, 0.0)
            total += jnp.where(shift_ref[r, (g + k) % G] == G - k, 1.0, 0.0)
        return total

    times_of = {k: times(k) for k in range(1, G)}

    def spread(value, box, send_sem, recv_sem, peer, n):
        box[0] = value
        for i in range(1, n):
            pltpu.make_async_remote_copy(
                src_ref=box.at[0], dst_ref=box.at[i], send_sem=send_sem.at[i - 1],
                recv_sem=recv_sem.at[i - 1], device_id=peer(i), device_id_type=MESH,
            ).start()

    def gathered(box, send_sem, recv_sem, peer, n):
        for i in range(1, n):
            pltpu.make_async_remote_copy(
                src_ref=box.at[0], dst_ref=box.at[i], send_sem=send_sem.at[i - 1],
                recv_sem=recv_sem.at[i - 1], device_id=peer(i), device_id_type=MESH,
            ).wait()
        return functools.reduce(jnp.add, [box[i] for i in range(n)])

    boxes = (
        (box_a, send_a, recv_a, peer_a, G * ZH),
        (box_b, send_b, recv_b, peer_b, Y),
        (box_c, send_c, recv_c, peer_c, X),
    )
    xts, cts, abs_ = (xt0, xt1), (ct0, ct1), (ab0, ab1)

    def ready(t, odd, i):
        scale = jnp.float32(1.0)
        for j, (axis, k) in enumerate(TILES):
            if axis == "grp":
                scale = jnp.where(t == j + 1, times_of[k], scale)
        prepare(blocks[t], scale, xts[odd], cts[odd], fs, t)
        abs_[odd][i, 0] = dot(xts[odd][...], ra[...])
        abs_[odd][i, 1] = dot(xts[odd][...], rb[...])

    def arrive(t):
        block_copy(t, visitor("blk", 1)).wait_recv()

    def energy_stage(t, odd, i, after):
        arrive(t + 1)
        ready(t + 1, 1 - odd, after)
        energy_pass(cts[odd], cj, abs_[odd], i, qk, t, eacc)

    ready(0, 0, 0)

    def energies(s, carry):
        energy_stage(2 * s, 0, s, s)
        energy_stage(2 * s + 1, 1, s, s + 1)
        eacc[...] = eacc[...] * jnp.where(s == 0, 0.5, 1.0)
        return carry

    lax.fori_loop(0, SAVED // 2, energies, 0)
    energy_stage(SAVED - 1, 0, SAVED // 2, SAVED // 2)
    e = jnp.sum(eacc[...], 0, keepdims=True)
    spread(functools.reduce(jnp.add, [e[:, k : k + 128] for k in range(0, count, 128)]), *boxes[0])

    def gradients(s, carry):
        for odd in range(2):
            t = 2 * s + odd
            grad_pass(saved_values(abs_[odd], s, qk, t), co, fs, t, jnp.maximum(t - 1, 0), acc, count)
        return carry

    lax.fori_loop(0, SAVED // 2, gradients, 0)
    grad_pass(saved_values(ab0, SAVED // 2, qk, SAVED - 1), co, fs, SAVED - 1, SAVED - 2, acc, count)

    spread(gathered(*boxes[0]), *boxes[1])

    def full_stage(t, odd, i, after):
        grad_pass(full_values(cts[odd], cj, abs_[odd], i), co, fs, t, t - 1, acc, count)

    arrive(SAVED + 1)
    ready(SAVED + 1, 0, 0)
    full_stage(SAVED, 1, SAVED // 2, 0)

    def rest(s, carry):
        t = SAVED + 1 + 2 * s

        @pl.when(s == 1)
        def _():
            spread(gathered(*boxes[1]), *boxes[2])

        arrive(t + 1)
        ready(t + 1, 1, 0)
        full_stage(t, 0, 0, 0)

        @pl.when(t + 2 < COUNT)
        def _():
            arrive(t + 2)

        ready(jnp.minimum(t + 2, COUNT - 1), 0, 0)
        full_stage(t + 1, 1, 0, 0)
        return carry

    lax.fori_loop(0, (COUNT - SAVED) // 2, rest, 0)
    reduce_chunk(co, count // CHUNK - 1, fs, COUNT - 1, acc)

    s = [acc[m, 0:8, :] + acc[m, 8:16, :] + acc[m, 16:24, :] for m in range(3)]
    twice = 2.0 * root
    gn = rows_of((own[0:3] * s[0][6:7] - s[0][0:3]) * twice)
    gc = (own[3:6] * s[0][6:7] + s[1][3:6]) * twice - 4.0 * (own[0:3] * s[2][6:7] - s[2][0:3])
    gc = gc / 3.0
    g1 = 0.5 * jnp.concatenate(cross(e2, gn), 0)
    g2 = 0.5 * jnp.concatenate(cross(gn, e1), 0)
    total = jnp.zeros((16, verts), F)
    for k, gu in enumerate((gc - g1 - g2, gc + g1, gc + g2)):
        parts = jnp.concatenate([*split3(gu), jnp.zeros((7, count), F)], 0).astype(B)
        total += lax.dot_general(parts, hot[k], (((1,), (1,)), ((), ())), preferred_element_type=F)
    grad_ref[...] = (total[0:3] + total[3:6] + total[6:9]) * (1.0 / count)

    for t in range(1, COUNT):
        block_copy(t, visitor(*TILES[t - 1])).wait_send()
    energy_ref[0] = jnp.sum(gathered(*boxes[2])) * (1.0 / (count * count * G * blk_n))


def shards(vertices, faces, trial_step, accepted, face_weight, partner_shift):
    verts, count = vertices.shape[1], faces.shape[1]
    hbm = pl.BlockSpec(memory_space=pltpu.HBM)
    dma = pltpu.SemaphoreType.DMA
    vmem = pltpu.VMEM
    slots = (SAVED + 1) // 2
    return tuple(pl.pallas_call(
        kernel,
        out_shape=(jax.ShapeDtypeStruct((3, verts), F), jax.ShapeDtypeStruct((1,), F)),
        in_specs=[hbm] * 6,
        out_specs=(
            pl.BlockSpec(memory_space=pltpu.VMEM), pl.BlockSpec(memory_space=pltpu.SMEM)
        ),
        scratch_shapes=[
            vmem((3, verts), F), vmem((3, count), jnp.int32), vmem((3, verts), F),
            vmem((1, count), F), pltpu.SMEM((1,), jnp.int32),
            pltpu.SMEM(partner_shift.shape, jnp.int32), dma((6,)),
            vmem((COUNT, 8, count), F),
            vmem((3, verts, count), B),
            vmem((count, 48), B), vmem((count, 48), B),
            vmem((count, 8), F), vmem((count, 8), F),
            vmem((COUNT, 64, count), B),
            vmem((48, count), B), vmem((48, count), B),
            vmem((3, 8, count), F),
            vmem((slots, 2, count, count), F), vmem((slots, 2, count, count), F),
            vmem((SAVED, 2, count, count), F),
            vmem((count // CHUNK, 6, CHUNK, count), B),
            vmem((3, 32, count), F),
            vmem((8, count), F),
            vmem((G * ZH, 1, 128), F), vmem((Y, 1, 128), F), vmem((X, 1, 128), F),
            dma((COUNT - 1,)), dma((COUNT - 1,)),
            dma((G * ZH - 1,)), dma((G * ZH - 1,)),
            dma((Y - 1,)), dma((Y - 1,)),
            dma((X - 1,)), dma((X - 1,)),
        ],
        compiler_params=pltpu.CompilerParams(
            collective_id=0, has_side_effects=True, vmem_limit_bytes=48 << 20
        ),
    )(vertices, faces, trial_step, face_weight.reshape(1, count), accepted, partner_shift))


def solution(mesh):
    both = ("grp", "blk")
    placed = (P(None, both), P(None, both), P(None, both), P("grp"), P(both), P())
    return jax.shard_map(
        shards, mesh=mesh, in_specs=placed, out_specs=(P(None, both), P()), check_vma=False
    )
```

```python
import functools

import jax
import jax.numpy as jnp
from jax import lax
from jax.experimental import pallas as pl
from jax.experimental.pallas import tpu as pltpu
from jax.sharding import PartitionSpec as P

F = jnp.float32
B = jnp.bfloat16
EPS2 = 0.05
HOPS = 4
CHUNK = 128
LANES = 256
ROWS = 16
MESH = pl.DeviceIdType.MESH
Y, ZH, X, G = 8, 4, 4, 4

TILES = (
    [("grp", 2), ("grp", 1)]
    + [("blk", k) for k in range(1, HOPS + 1)]
    + [("grp", 3)]
    + [("blk", -k) for k in range(1, HOPS + 1)]
)
COUNT = len(TILES) + 1
HALF_AT = 2
FULL_AT = 7
PASS_AT = 9


def split3(x):
    h = x.astype(B).astype(F)
    r = x - h
    m = r.astype(B).astype(F)
    return h, m, r - m


def dot(a, b):
    return jnp.dot(a, b, preferred_element_type=F)


def cross(a, b):
    return [
        a[1] * b[2] - a[2] * b[1],
        a[2] * b[0] - a[0] * b[2],
        a[0] * b[1] - a[1] * b[0],
    ]


def rows_of(x, n=3):
    return [x[k : k + 1] for k in range(n)]


def own_prep(own, ra, rb, cj):
    n = own.shape[1]
    z = jnp.zeros((1, n), F)
    ya = jnp.concatenate([-own[3:6], z, z, z, own[7:8], z], 0)
    yb = jnp.concatenate([z, z, z, own[0:3], z, z - 1.0], 0)
    for y, r in ((ya, ra), (yb, rb)):
        h, m, low = split3(y)
        r[...] = jnp.concatenate([h, m, low, h, m, h], 0).astype(B)
    for k in range(3):
        cj[k] = jnp.broadcast_to(own[k : k + 1], (8, n))


def other_prep(blk, wrow, xt, ct, fs, slot):
    row = lax.broadcasted_iota(jnp.int32, blk.shape, 0)
    x = jnp.where(row == 6, 1.0, blk)
    h, m, low = split3(x)
    xt[slot] = jnp.concatenate([h, h, h, m, m, low], 0).astype(B).T
    ct[slot] = blk.T
    h, m, low = split3(x * wrow)
    fs[slot] = jnp.concatenate([h, m, low, jnp.zeros_like(low)], 0).astype(B)


def pairs(ct, cj, ab, co, slot, base, r0):
    n = cj.shape[2]
    rows = slice(base + r0, base + r0 + ROWS)
    cr = slice(r0, r0 + ROWS)
    for l0 in range(0, n, LANES):
        ls = slice(l0, l0 + LANES)
        d = []
        for k in range(3):
            other = jnp.broadcast_to(ct[rows, k : k + 1], (ROWS, LANES))
            own = cj[k, :, ls]
            d.append(jnp.concatenate([own] * (ROWS // 8), 0) - other)
        q = 1.0 / ((d[0] * d[0] + EPS2) + (d[1] * d[1] + d[2] * d[2]))
        q2 = q * q
        a = ab[slot, 0, cr, ls]
        b = ab[slot, 1, cr, ls]
        al = a * q2
        be = b * q2
        ga = (a * al + b * be) * q
        for m, v in enumerate((al, be, ga)):
            h = v.astype(B)
            co[slot, 2 * m, cr, ls] = h
            co[slot, 2 * m + 1, cr, ls] = (v - h.astype(F)).astype(B)


def tile(xt, ct, fs, ra, rb, cj, ab, co, acc):
    chunks = cj.shape[2] // CHUNK

    def project(c):
        x = xt[c * CHUNK : (c + 1) * CHUNK, :]
        ab[c % 2, 0] = dot(x, ra[...])
        ab[c % 2, 1] = dot(x, rb[...])

    project(0)
    for c in range(chunks):
        if c + 1 < chunks:
            project(c + 1)
        for r0 in range(0, CHUNK, ROWS):
            pairs(ct, cj, ab, co, c % 2, c * CHUNK, r0)
        f = fs[:, c * CHUNK : (c + 1) * CHUNK]
        for m in range(3):
            acc[m] += dot(f, co[c % 2, 2 * m]) + dot(f, co[c % 2, 2 * m + 1])


def sums_of(acc):
    return [acc[m, 0:8, :] + acc[m, 8:16, :] + acc[m, 16:24, :] for m in range(3)]


def grad_normal(own, s):
    return own[0:3] * s[0][6:7] - s[0][0:3]


def energy_of(own, acc):
    s = sums_of(acc)
    e = jnp.sum(own[3:6] * grad_normal(own, s) + own[0:3] * s[1][3:6], 0, keepdims=True)
    e = (e - s[1][7:8]) * own[6:7]
    n = e.shape[1]
    return functools.reduce(jnp.add, [e[:, k : k + 128] for k in range(0, n, 128)])


def kernel(
    ver_hbm, faces_hbm, step_hbm, weight_hbm, acc_hbm, shift_hbm, grad_ref, energy_ref,
    ver_ref, faces_ref, step_ref, weight_ref, acc_ref, shift_ref, in_sem,
    blocks, hot, xt, ct, fs, ra, rb, cj, ab, co, acc, part,
    box_a, box_b, send, recv, send_a, recv_a, send_b, recv_b,
):
    g = lax.axis_index("grp")
    b = lax.axis_index("blk")
    blk_n = Y * ZH * X
    y, zh, x = b // (ZH * X), (b // X) % ZH, b % X

    def peer_a(i):
        j = (g * ZH + zh + i) % (G * ZH)
        return (j // ZH, (y * ZH + j % ZH) * X + x)

    def peer_b(i):
        j = (y * X + x + i) % (Y * X)
        return (g, ((j // X) * ZH + zh) * X + j % X)

    def visitor(axis, k):
        if axis == "grp":
            return ((g + G - k) % G, b)
        return (g, (b + blk_n - k) % blk_n)

    peers = [visitor(*t) for t in TILES if t[0] == "blk"]
    peers += [peer_a(i) for i in range(1, G * ZH)]
    peers += [peer_b(i) for i in range(1, Y * X)]
    barrier = pltpu.get_barrier_semaphore()
    for p in peers:
        pl.semaphore_signal(barrier, inc=1, device_id=p, device_id_type=MESH)

    loads = [
        pltpu.make_async_copy(src, dst, in_sem.at[i])
        for i, (src, dst) in enumerate((
            (ver_hbm, ver_ref), (step_hbm, step_ref), (faces_hbm, faces_ref),
            (weight_hbm, weight_ref), (acc_hbm, acc_ref), (shift_hbm, shift_ref),
        ))
    ]
    for c in loads:
        c.start()
    acc[...] = jnp.zeros_like(acc)
    for c in loads:
        c.wait()

    verts, count = ver_ref.shape[1], faces_ref.shape[1]
    pos = ver_ref[...] + acc_ref[0].astype(F) * step_ref[...]
    table = jnp.concatenate([*split3(pos), jnp.zeros((7, verts), F)], 0).astype(B)
    vert = lax.broadcasted_iota(jnp.int32, (verts, count), 0)
    corners = []
    for k in range(3):
        hot[k] = jnp.where(vert == faces_ref[k : k + 1, :], 1.0, 0.0).astype(B)
        u = dot(table, hot[k])
        corners.append(u[0:3] + u[3:6] + u[6:9])
    center = (corners[0] + corners[1] + corners[2]) / 3.0
    e1 = rows_of(corners[1] - corners[0])
    e2 = rows_of(corners[2] - corners[0])
    normal = 0.5 * jnp.concatenate(cross(e1, e2), 0)
    offset = jnp.sum(center * normal, 0, keepdims=True)
    own = jnp.concatenate([center, normal, weight_ref[...], offset], 0)
    blocks[0] = own

    pl.semaphore_wait(barrier, len(peers))

    def block_copy(t, to):
        return pltpu.make_async_remote_copy(
            src_ref=blocks.at[0], dst_ref=blocks.at[t], send_sem=send.at[t - 1],
            recv_sem=recv.at[t - 1], device_id=to, device_id_type=MESH,
        )

    for t, where in enumerate(TILES):
        block_copy(t + 1, visitor(*where)).start()

    own_prep(own, ra, rb, cj)

    def times(k):
        total = jnp.float32(0.0)
        for r in range(shift_ref.shape[0]):
            total += jnp.where(shift_ref[r, g] == k, 1.0, 0.0)
            total += jnp.where(shift_ref[r, (g + k) % G] == G - k, 1.0, 0.0)
        return total

    times_of = {k: times(k) for k in range(1, G)}

    def spread(value, box, send_sem, recv_sem, peer, n):
        box[0] = value
        for i in range(1, n):
            pltpu.make_async_remote_copy(
                src_ref=box.at[0], dst_ref=box.at[i], send_sem=send_sem.at[i - 1],
                recv_sem=recv_sem.at[i - 1], device_id=peer(i), device_id_type=MESH,
            ).start()

    def gathered(box, send_sem, recv_sem, peer, n):
        for i in range(1, n):
            pltpu.make_async_remote_copy(
                src_ref=box.at[0], dst_ref=box.at[i], send_sem=send_sem.at[i - 1],
                recv_sem=recv_sem.at[i - 1], device_id=peer(i), device_id_type=MESH,
            ).wait()
        return functools.reduce(jnp.add, [box[i] for i in range(n)])

    boxes = (
        (box_a, send_a, recv_a, peer_a, G * ZH),
        (box_b, send_b, recv_b, peer_b, Y * X),
    )

    def ready(t):
        scale = jnp.float32(1.0)
        for j, (axis, k) in enumerate(TILES):
            if axis == "grp":
                scale = jnp.where(t == j + 1, times_of[k], scale)
        blk = blocks[t]
        other_prep(blk, blk[6:7] * scale, xt, ct, fs, t % 2)

    def visit(t, carry):
        @pl.when(t + 1 < COUNT)
        def _():
            block_copy(t + 1, visitor("blk", 1)).wait_recv()

        @pl.when(t == HALF_AT)
        def _():
            part[...] = energy_of(own, acc)

        @pl.when(t == FULL_AT)
        def _():
            spread(energy_of(own, acc) - 0.5 * part[...], *boxes[0])

        @pl.when(t == PASS_AT)
        def _():
            spread(gathered(*boxes[0]), *boxes[1])

        now = t % 2
        tile(xt.at[now], ct.at[now], fs.at[now], ra, rb, cj, ab, co, acc)
        ready(jnp.minimum(t + 1, COUNT - 1))
        return carry

    ready(0)
    lax.fori_loop(0, COUNT, visit, 0)

    s = sums_of(acc)
    twice = 2.0 * own[6:7]
    gn = rows_of(grad_normal(own, s) * twice)
    gc = own[3:6] * s[0][6:7] + s[1][3:6] - 2.0 * (own[0:3] * s[2][6:7] - s[2][0:3])
    gc = gc * (twice / 3.0)
    g1 = 0.5 * jnp.concatenate(cross(e2, gn), 0)
    g2 = 0.5 * jnp.concatenate(cross(gn, e1), 0)
    total = jnp.zeros((16, verts), F)
    for k, gu in enumerate((gc - g1 - g2, gc + g1, gc + g2)):
        parts = jnp.concatenate([*split3(gu), jnp.zeros((7, count), F)], 0).astype(B)
        total += lax.dot_general(parts, hot[k], (((1,), (1,)), ((), ())), preferred_element_type=F)
    grad_ref[...] = (total[0:3] + total[3:6] + total[6:9]) * (1.0 / count)

    for t, where in enumerate(TILES):
        block_copy(t + 1, visitor(*where)).wait_send()
    energy_ref[0] = jnp.sum(gathered(*boxes[1])) * (1.0 / (count * count * G * blk_n))


def shards(vertices, faces, trial_step, accepted, face_weight, partner_shift):
    verts, count = vertices.shape[1], faces.shape[1]
    hbm = pl.BlockSpec(memory_space=pltpu.HBM)
    dma = pltpu.SemaphoreType.DMA
    vmem = pltpu.VMEM
    return tuple(pl.pallas_call(
        kernel,
        out_shape=(jax.ShapeDtypeStruct((3, verts), F), jax.ShapeDtypeStruct((1,), F)),
        in_specs=[hbm] * 6,
        out_specs=(
            pl.BlockSpec(memory_space=pltpu.VMEM), pl.BlockSpec(memory_space=pltpu.SMEM)
        ),
        scratch_shapes=[
            vmem((3, verts), F), vmem((3, count), jnp.int32), vmem((3, verts), F),
            vmem((1, count), F), pltpu.SMEM((1,), jnp.int32),
            pltpu.SMEM(partner_shift.shape, jnp.int32), dma((6,)),
            vmem((COUNT, 8, count), F),
            vmem((3, verts, count), B),
            vmem((2, count, 48), B),
            vmem((2, count, 8), F),
            vmem((2, 32, count), B),
            vmem((48, count), B), vmem((48, count), B),
            vmem((3, 8, count), F),
            vmem((2, 2, CHUNK, count), F),
            vmem((2, 6, CHUNK, count), B),
            vmem((3, 32, count), F),
            vmem((1, 128), F),
            vmem((G * ZH, 1, 128), F), vmem((Y * X, 1, 128), F),
            dma((COUNT - 1,)), dma((COUNT - 1,)),
            dma((G * ZH - 1,)), dma((G * ZH - 1,)),
            dma((Y * X - 1,)), dma((Y * X - 1,)),
        ],
        compiler_params=pltpu.CompilerParams(collective_id=0, has_side_effects=True),
    )(vertices, faces, trial_step, face_weight.reshape(1, count), accepted, partner_shift))


def solution(mesh):
    both = ("grp", "blk")
    placed = (P(None, both), P(None, both), P(None, both), P("grp"), P(both), P())
    return jax.shard_map(
        shards, mesh=mesh, in_specs=placed, out_specs=(P(None, both), P()), check_vma=False
    )
```

```python
import functools

import jax
import jax.numpy as jnp
from jax import lax
from jax.experimental import pallas as pl
from jax.experimental.pallas import tpu as pltpu
from jax.sharding import PartitionSpec as P

F = jnp.float32
B = jnp.bfloat16
EPS2 = 0.05
HOPS = 4
CHUNK = 128
LANES = 256
ROWS = 16
MESH = pl.DeviceIdType.MESH
Y, ZH, X, G = 8, 4, 4, 4

TILES = (
    [("grp", 2), ("grp", 1)]
    + [("blk", k) for k in range(1, HOPS + 1)]
    + [("grp", 3)]
    + [("blk", -k) for k in range(1, HOPS + 1)]
)
COUNT = len(TILES) + 1
HALF_AT = 2
FULL_AT = 7
PASS_AT = 9


def split3(x):
    h = x.astype(B).astype(F)
    r = x - h
    m = r.astype(B).astype(F)
    return h, m, r - m


def dot(a, b):
    return jnp.dot(a, b, preferred_element_type=F)


def cross(a, b):
    return [
        a[1] * b[2] - a[2] * b[1],
        a[2] * b[0] - a[0] * b[2],
        a[0] * b[1] - a[1] * b[0],
    ]


def rows_of(x, n=3):
    return [x[k : k + 1] for k in range(n)]


def own_prep(own, ra, rb, cj):
    n = own.shape[1]
    z = jnp.zeros((1, n), F)
    ya = jnp.concatenate([-own[3:6], z, z, z, own[7:8], z], 0)
    yb = jnp.concatenate([z, z, z, own[0:3], z, z - 1.0], 0)
    for y, r in ((ya, ra), (yb, rb)):
        h, m, low = split3(y)
        r[...] = jnp.concatenate([h, m, low, h, m, h], 0).astype(B)
    for k in range(3):
        cj[k] = jnp.broadcast_to(own[k : k + 1], (8, n))


def other_prep(blk, wrow, xt, ct, fs, slot):
    row = lax.broadcasted_iota(jnp.int32, blk.shape, 0)
    x = jnp.where(row == 6, 1.0, blk)
    h, m, low = split3(x)
    xt[slot] = jnp.concatenate([h, h, h, m, m, low], 0).astype(B).T
    ct[slot] = blk.T
    h, m, low = split3(x * wrow)
    fs[slot] = jnp.concatenate([h, m, low, jnp.zeros_like(low)], 0).astype(B)


def pairs(ct, cj, ab, co, slot, base, r0):
    n = cj.shape[2]
    rows = slice(base + r0, base + r0 + ROWS)
    cr = slice(r0, r0 + ROWS)
    for l0 in range(0, n, LANES):
        ls = slice(l0, l0 + LANES)
        d = []
        for k in range(3):
            other = jnp.broadcast_to(ct[rows, k : k + 1], (ROWS, LANES))
            own = cj[k, :, ls]
            d.append(jnp.concatenate([own] * (ROWS // 8), 0) - other)
        q = 1.0 / ((d[0] * d[0] + EPS2) + (d[1] * d[1] + d[2] * d[2]))
        q2 = q * q
        a = ab[slot, 0, cr, ls]
        b = ab[slot, 1, cr, ls]
        al = a * q2
        be = b * q2
        ga = (a * al + b * be) * q
        for m, v in enumerate((al, be, ga)):
            h = v.astype(B)
            co[slot, 2 * m, cr, ls] = h
            co[slot, 2 * m + 1, cr, ls] = (v - h.astype(F)).astype(B)


def tile(xt, ct, fs, ra, rb, cj, ab, co, acc):
    chunks = cj.shape[2] // CHUNK

    def project(c):
        x = xt[c * CHUNK : (c + 1) * CHUNK, :]
        ab[c % 2, 0] = dot(x, ra[...])
        ab[c % 2, 1] = dot(x, rb[...])

    project(0)
    for c in range(chunks):
        if c + 1 < chunks:
            project(c + 1)
        for r0 in range(0, CHUNK, ROWS):
            pairs(ct, cj, ab, co, c % 2, c * CHUNK, r0)
        f = fs[:, c * CHUNK : (c + 1) * CHUNK]
        for m in range(3):
            acc[m] += dot(f, co[c % 2, 2 * m]) + dot(f, co[c % 2, 2 * m + 1])


def sums_of(acc):
    return [acc[m, 0:8, :] + acc[m, 8:16, :] + acc[m, 16:24, :] for m in range(3)]


def grad_normal(own, s):
    return own[0:3] * s[0][6:7] - s[0][0:3]


def energy_of(own, acc):
    s = sums_of(acc)
    e = jnp.sum(own[3:6] * grad_normal(own, s) + own[0:3] * s[1][3:6], 0, keepdims=True)
    e = (e - s[1][7:8]) * own[6:7]
    n = e.shape[1]
    return functools.reduce(jnp.add, [e[:, k : k + 128] for k in range(0, n, 128)])


def kernel(
    ver_hbm, faces_hbm, step_hbm, weight_hbm, acc_hbm, shift_hbm, grad_ref, energy_ref,
    ver_ref, faces_ref, step_ref, weight_ref, acc_ref, shift_ref, in_sem,
    blocks, hot, xt, ct, fs, ra, rb, cj, ab, co, acc, part,
    box_a, box_b, box_c, send, recv, send_a, recv_a, send_b, recv_b, send_c, recv_c,
):
    g = lax.axis_index("grp")
    b = lax.axis_index("blk")
    blk_n = Y * ZH * X
    y, zh, x = b // (ZH * X), (b // X) % ZH, b % X

    def peer_a(i):
        j = (g * ZH + zh + i) % (G * ZH)
        return (j // ZH, (y * ZH + j % ZH) * X + x)

    def peer_b(i):
        return (g, (((y + i) % Y) * ZH + zh) * X + x)

    def peer_c(i):
        return (g, (y * ZH + zh) * X + (x + i) % X)

    def visitor(axis, k):
        if axis == "grp":
            return ((g + G - k) % G, b)
        return (g, (b + blk_n - k) % blk_n)

    peers = [visitor(*t) for t in TILES if t[0] == "blk"]
    peers += [peer_a(i) for i in range(1, G * ZH)]
    peers += [peer_b(i) for i in range(1, Y)] + [peer_c(i) for i in range(1, X)]
    barrier = pltpu.get_barrier_semaphore()
    for p in peers:
        pl.semaphore_signal(barrier, inc=1, device_id=p, device_id_type=MESH)

    loads = [
        pltpu.make_async_copy(src, dst, in_sem.at[i])
        for i, (src, dst) in enumerate((
            (ver_hbm, ver_ref), (step_hbm, step_ref), (faces_hbm, faces_ref),
            (weight_hbm, weight_ref), (acc_hbm, acc_ref), (shift_hbm, shift_ref),
        ))
    ]
    for c in loads:
        c.start()
    acc[...] = jnp.zeros_like(acc)
    for c in loads:
        c.wait()

    verts, count = ver_ref.shape[1], faces_ref.shape[1]
    pos = ver_ref[...] + acc_ref[0].astype(F) * step_ref[...]
    table = jnp.concatenate([*split3(pos), jnp.zeros((7, verts), F)], 0).astype(B)
    vert = lax.broadcasted_iota(jnp.int32, (verts, count), 0)
    corners = []
    for k in range(3):
        hot[k] = jnp.where(vert == faces_ref[k : k + 1, :], 1.0, 0.0).astype(B)
        u = dot(table, hot[k])
        corners.append(u[0:3] + u[3:6] + u[6:9])
    center = (corners[0] + corners[1] + corners[2]) / 3.0
    e1 = rows_of(corners[1] - corners[0])
    e2 = rows_of(corners[2] - corners[0])
    normal = 0.5 * jnp.concatenate(cross(e1, e2), 0)
    offset = jnp.sum(center * normal, 0, keepdims=True)
    own = jnp.concatenate([center, normal, weight_ref[...], offset], 0)
    blocks[0] = own

    pl.semaphore_wait(barrier, len(peers))

    def block_copy(t, to):
        return pltpu.make_async_remote_copy(
            src_ref=blocks.at[0], dst_ref=blocks.at[t], send_sem=send.at[t - 1],
            recv_sem=recv.at[t - 1], device_id=to, device_id_type=MESH,
        )

    for t, where in enumerate(TILES):
        block_copy(t + 1, visitor(*where)).start()

    own_prep(own, ra, rb, cj)

    def times(k):
        total = jnp.float32(0.0)
        for r in range(shift_ref.shape[0]):
            total += jnp.where(shift_ref[r, g] == k, 1.0, 0.0)
            total += jnp.where(shift_ref[r, (g + k) % G] == G - k, 1.0, 0.0)
        return total

    times_of = {k: times(k) for k in range(1, G)}

    def spread(value, box, send_sem, recv_sem, peer, n):
        box[0] = value
        for i in range(1, n):
            pltpu.make_async_remote_copy(
                src_ref=box.at[0], dst_ref=box.at[i], send_sem=send_sem.at[i - 1],
                recv_sem=recv_sem.at[i - 1], device_id=peer(i), device_id_type=MESH,
            ).start()

    def gathered(box, send_sem, recv_sem, peer, n):
        for i in range(1, n):
            pltpu.make_async_remote_copy(
                src_ref=box.at[0], dst_ref=box.at[i], send_sem=send_sem.at[i - 1],
                recv_sem=recv_sem.at[i - 1], device_id=peer(i), device_id_type=MESH,
            ).wait()
        return functools.reduce(jnp.add, [box[i] for i in range(n)])

    boxes = (
        (box_a, send_a, recv_a, peer_a, G * ZH),
        (box_b, send_b, recv_b, peer_b, Y),
        (box_c, send_c, recv_c, peer_c, X),
    )

    def ready(t):
        scale = jnp.float32(1.0)
        for j, (axis, k) in enumerate(TILES):
            if axis == "grp":
                scale = jnp.where(t == j + 1, times_of[k], scale)
        blk = blocks[t]
        other_prep(blk, blk[6:7] * scale, xt, ct, fs, t % 2)

    def visit(t, carry):
        @pl.when(t + 1 < COUNT)
        def _():
            block_copy(t + 1, visitor("blk", 1)).wait_recv()

        @pl.when(t == HALF_AT)
        def _():
            part[...] = energy_of(own, acc)

        @pl.when(t == FULL_AT)
        def _():
            spread(energy_of(own, acc) - 0.5 * part[...], *boxes[0])

        @pl.when(t == PASS_AT)
        def _():
            spread(gathered(*boxes[0]), *boxes[1])

        @pl.when(t == PASS_AT + 2)
        def _():
            spread(gathered(*boxes[1]), *boxes[2])

        now = t % 2
        tile(xt.at[now], ct.at[now], fs.at[now], ra, rb, cj, ab, co, acc)
        ready(jnp.minimum(t + 1, COUNT - 1))
        return carry

    ready(0)
    lax.fori_loop(0, COUNT, visit, 0)

    s = sums_of(acc)
    twice = 2.0 * own[6:7]
    gn = rows_of(grad_normal(own, s) * twice)
    gc = own[3:6] * s[0][6:7] + s[1][3:6] - 2.0 * (own[0:3] * s[2][6:7] - s[2][0:3])
    gc = gc * (twice / 3.0)
    g1 = 0.5 * jnp.concatenate(cross(e2, gn), 0)
    g2 = 0.5 * jnp.concatenate(cross(gn, e1), 0)
    total = jnp.zeros((16, verts), F)
    for k, gu in enumerate((gc - g1 - g2, gc + g1, gc + g2)):
        parts = jnp.concatenate([*split3(gu), jnp.zeros((7, count), F)], 0).astype(B)
        total += lax.dot_general(parts, hot[k], (((1,), (1,)), ((), ())), preferred_element_type=F)
    grad_ref[...] = (total[0:3] + total[3:6] + total[6:9]) * (1.0 / count)

    for t, where in enumerate(TILES):
        block_copy(t + 1, visitor(*where)).wait_send()
    energy_ref[0] = jnp.sum(gathered(*boxes[2])) * (1.0 / (count * count * G * blk_n))


def shards(vertices, faces, trial_step, accepted, face_weight, partner_shift):
    verts, count = vertices.shape[1], faces.shape[1]
    hbm = pl.BlockSpec(memory_space=pltpu.HBM)
    dma = pltpu.SemaphoreType.DMA
    vmem = pltpu.VMEM
    return tuple(pl.pallas_call(
        kernel,
        out_shape=(jax.ShapeDtypeStruct((3, verts), F), jax.ShapeDtypeStruct((1,), F)),
        in_specs=[hbm] * 6,
        out_specs=(
            pl.BlockSpec(memory_space=pltpu.VMEM), pl.BlockSpec(memory_space=pltpu.SMEM)
        ),
        scratch_shapes=[
            vmem((3, verts), F), vmem((3, count), jnp.int32), vmem((3, verts), F),
            vmem((1, count), F), pltpu.SMEM((1,), jnp.int32),
            pltpu.SMEM(partner_shift.shape, jnp.int32), dma((6,)),
            vmem((COUNT, 8, count), F),
            vmem((3, verts, count), B),
            vmem((2, count, 48), B),
            vmem((2, count, 8), F),
            vmem((2, 32, count), B),
            vmem((48, count), B), vmem((48, count), B),
            vmem((3, 8, count), F),
            vmem((2, 2, CHUNK, count), F),
            vmem((2, 6, CHUNK, count), B),
            vmem((3, 32, count), F),
            vmem((1, 128), F),
            vmem((G * ZH, 1, 128), F), vmem((Y, 1, 128), F), vmem((X, 1, 128), F),
            dma((COUNT - 1,)), dma((COUNT - 1,)),
            dma((G * ZH - 1,)), dma((G * ZH - 1,)),
            dma((Y - 1,)), dma((Y - 1,)),
            dma((X - 1,)), dma((X - 1,)),
        ],
        compiler_params=pltpu.CompilerParams(collective_id=0, has_side_effects=True),
    )(vertices, faces, trial_step, face_weight.reshape(1, count), accepted, partner_shift))


def solution(mesh):
    both = ("grp", "blk")
    placed = (P(None, both), P(None, both), P(None, both), P("grp"), P(both), P())
    return jax.shard_map(
        shards, mesh=mesh, in_specs=placed, out_specs=(P(None, both), P()), check_vma=False
    )
```
